256 devices in a mesh: seq: 16 (over z, x_lo), wr: 4 (over y), wc: 4 (over x_hi, core).
Axes of the slice: x: 4 (x_hi: 2, x_lo: 2; x = x_hi * 2 + x_lo), y: 4, z: 8, core: 2. Of those that a mesh axis runs over, the one named last changes fastest.
Arguments:
- tokens: bfloat16 [8192, 2048], P('seq', ('wr', 'wc')), may hold values from -6 to 6
- ln_gain: float32 [2, 2048], replicated, may hold values from 0.5 to 1.5
- w_branch: bfloat16 [2, 2048, 4096], P(None, None, ('wr', 'wc')), may hold values from -0.125 to 0.125
- w_outgate: bfloat16 [2, 2048, 4096], P(None, None, ('wr', 'wc')), may hold values from -0.125 to 0.125
- w_gates: bfloat16 [2, 2048, 8], replicated, may hold values from -0.125 to 0.125
- forget_bias: float32 [2, 4], replicated, may hold values from 3.2 to 11
- conv_weight: float32 [2, 4, 4096], P(None, None, ('wr', 'wc')), may hold values from -3 to 3
- conv_bias: float32 [2, 4096], P(None, ('wr', 'wc')), may hold values from -3 to 3
- w_query: float32 [2, 4, 4, 4, 256], P(None, 'wr'), may hold values from -3 to 3
- w_key: float32 [2, 4, 4, 4, 256], P(None, 'wr'), may hold values from -3 to 3
- w_value: float32 [2, 4, 4, 4, 256], P(None, 'wr', None, 'wc'), may hold values from -4 to 4
- skip_gain: float32 [2, 4096], P(None, ('wr', 'wc')), may hold values from 0.5 to 1.5
- norm_gain: float32 [2, 4096], P(None, ('wr', 'wc')), may hold values from 0.5 to 1.5
- w_down: bfloat16 [2, 4096, 2048], P(None, ('wr', 'wc')), may hold values from -0.125 to 0.125
- lengths: int32 [3], replicated, may hold values from 1 to 4096, 8192 in all
- request_prompt: int32 [32], P('seq'), may hold values from 0 to 2
Outputs:
- mixed: bfloat16 [8192, 2048], P('seq', ('wr', 'wc'))
- request_state: bfloat16 [2, 32, 4, 1024, 1024], P(None, 'seq', 'wr', None, 'wc')
- request_conv: bfloat16 [2, 32, 3, 4096], P(None, 'seq', None, ('wr', 'wc'))
The draws below stay inside these ranges and needn't reach their ends.
Inputs may be any that keep to these rules, and one draw needn't show every extreme that they name: `lengths`: the 3 prompts lie end to end in order and fill all 8192 positions; the longest has exactly 4096 positions.
All inputs are finite; a program needn't handle non-finite values.
Results may differ from the reference program's by a relative error of at most 0.035.
Values may be sent and summed in bfloat16 or wider, within the bound.
A program may use at most 128 MiB of HBM per device.

```python
import math
import jax
import jax.numpy as jnp
import numpy as np
from jax import lax

D = 2048
INNER = 4096
HEADS = 4
CONV = 4
LAYERS = 2
BLK = 512
PROMPTS = 3
TOK_DEV = 512
QB = 256
TOKENS = 8192
REQS = 32
MOSTLEN = 4096
N_WR = 4
N_WC = 4


def draw_forget_bias(key, part):
    slow_key, fast_key, pick_key = jax.random.split(key, 3)
    slow_rate = jax.random.uniform(slow_key, (LAYERS, HEADS), jnp.float32, 9.0, 11.0)
    fast_rate = jax.random.uniform(fast_key, (LAYERS, HEADS), jnp.float32, 3.2, 5.0)
    chooser = jax.random.uniform(pick_key, (LAYERS, HEADS), jnp.float32)
    picked = jnp.where(chooser < 0.5, slow_rate, fast_rate)
    return picked


def draw_w_value(key, part):
    base_key = jax.random.fold_in(key, 0)
    draw_shape = (LAYERS, HEADS, 4, 4, QB)
    column = jnp.arange(4, dtype=jnp.float32).reshape(1, 1, 1, 4, 1)
    rising = 0.6 + 0.4 * column
    sampled = 0.5 * jax.random.normal(base_key, draw_shape, jnp.float32) * rising
    return jnp.clip(sampled, -4.0, 4.0)


def with_ends(entries, rng, smallest, top_value):
    index_at = [jax.random.randint(jax.random.fold_in(rng, axis), (), 0, length) for axis, length in enumerate(entries.shape)]
    widest = entries.shape.index(max(entries.shape))
    neighbour = index_at[:widest] + [(index_at[widest] + 1) % entries.shape[widest]] + index_at[widest + 1:]
    return entries.at[tuple(index_at)].set(smallest).at[tuple(neighbour)].set(top_value)


def strengthened(drawn, stream_key, source, target, shards_of, factor):
    def block_of(position):
        return (jnp.arange(drawn.shape[position]) // (drawn.shape[position] // shards_of)).reshape((-1,) + (1,) * (drawn.ndim - 1 - position))

    first = jax.random.permutation(stream_key, shards_of)[block_of(target)]
    far = (block_of(target) + shards_of // 2) % shards_of
    return jnp.where((block_of(source) == first) | (block_of(source) == far), factor * drawn, drawn)


def shard_levels(rng, shape, pieces, least, high):
    level = 1.0
    for dim, blocks in pieces:
        heights = jax.random.uniform(jax.random.fold_in(jax.random.fold_in(rng, 6), dim), (blocks,), jnp.float32, least / len(pieces), high / len(pieces))
        level = level * jnp.repeat(jnp.exp(heights), shape[dim] // blocks).reshape((-1,) + (1,) * (len(shape) - 1 - dim))
    return level


def profile(count, total, limit, lean):
    weights = [(1 << 20) // math.isqrt(standing ** lean) + 1 for standing in range(2, count + 1)]
    surplus, given = total - limit - (count - 1), [1] * (count - 1)
    while surplus > 0:
        free = [i for i in range(count - 1) if given[i] < limit]
        whole, left = sum([weights[i] for i in free]), surplus
        for i in free:
            more = min(limit - given[i], max(1, left * weights[i] // whole), surplus)
            given[i] = given[i] + more
            surplus = surplus - more
    return np.array([limit] + given)


def ragged(key, amount, total, most, slope):
    if amount == 2:
        one = jax.random.randint(key, (), max(1, total - most), min(most, total - 1) + 1)
        return jnp.stack([one, total - one])
    sizes = jnp.asarray(profile(amount, total, most, slope), jnp.int32)
    twos = (amount - 1) // 2
    source_of, taker = sizes[1:1 + 2 * twos:2], sizes[2:2 + 2 * twos:2]
    slack = jnp.minimum(source_of - 1, most - taker)
    moved = jax.random.randint(jax.random.fold_in(key, 1), (twos,), 0, 1 << 20) % (slack + 1)
    sizes = sizes.at[1:1 + 2 * twos:2].set(source_of - moved).at[2:2 + 2 * twos:2].set(taker + moved)
    return sizes[jax.random.permutation(jax.random.fold_in(key, 2), amount)]


def scatter_about(stream_key, extent, deviation, limit, cuts=(), kind=jnp.bfloat16):
    result = jax.random.normal(stream_key, extent, jnp.float32) * deviation
    if len(cuts) > 0:
        result = shard_levels(stream_key, extent, cuts, -0.22, 0.18) * result
    return jnp.clip(result, min=-limit, max=limit).astype(kind)


def gaussian_with(own_key, extent, scale, limit, cuts, heavy, kind=jnp.bfloat16):
    result = scale * jax.random.normal(own_key, extent, jnp.float32)
    if cuts:
        result = result * shard_levels(own_key, extent, cuts, -0.22, 0.18)
    return jnp.clip(strengthened(result, jax.random.fold_in(own_key, 3), *heavy), -limit, limit).astype(kind)


def setup_inputs(seed: int = 0) -> dict:
    splits = jax.random.split(jax.random.key(seed), 17)
    tokens = scatter_about(splits[0], (TOKENS, D), 1.0, 6.0, ((0, 16), (1, 16)))
    ln_gain = jnp.clip(1.0 + 0.1 * jax.random.normal(splits[1], (LAYERS, D), jnp.float32), 0.5, 1.5)
    w_branch = scatter_about(splits[2], (LAYERS, D, INNER), D ** -0.5, 0.125, ((2, 16),))
    w_outgate = scatter_about(splits[3], (LAYERS, D, INNER), D ** -0.5, 0.125, ((2, 16),))
    w_gates = scatter_about(splits[4], (LAYERS, D, 2 * HEADS), D ** -0.5, 0.125)
    forget_bias = draw_forget_bias(jax.random.fold_in(splits[16], 71), 0)
    conv_weight = scatter_about(splits[6], (LAYERS, CONV, INNER), CONV ** -0.5, 3.0, ((2, 16),), jnp.float32)
    conv_bias = scatter_about(splits[7], (LAYERS, INNER), 0.5, 3.0, ((1, 16),), jnp.float32)
    w_query = scatter_about(splits[8], (LAYERS, HEADS, 4, 4, QB), 4 ** -0.5, 3.0, ((1, 4),), jnp.float32)
    w_key = scatter_about(splits[9], (LAYERS, HEADS, 4, 4, QB), 4 ** -0.5, 3.0, ((1, 4),), jnp.float32)
    w_value = draw_w_value(jax.random.fold_in(splits[16], 71), 0)
    skip_gain = jnp.clip(1.0 + 0.1 * jax.random.normal(splits[11], (LAYERS, INNER), jnp.float32), 0.5, 1.5)
    norm_gain = jnp.clip(1.0 + 0.1 * jax.random.normal(splits[12], (LAYERS, INNER), jnp.float32), 0.5, 1.5)
    w_down = gaussian_with(splits[13], (LAYERS, INNER, D), INNER ** -0.5, 0.125, ((1, 16),), (1, 2, 16, 2.0))
    lengths = ragged(splits[14], PROMPTS, TOKENS, MOSTLEN, 1).astype(jnp.int32)
    request_prompt = with_ends(jax.random.randint(splits[15], (REQS,), 0, PROMPTS), jax.random.fold_in(splits[15], 1), 0, PROMPTS - 1).astype(jnp.int32)
    return {"tokens": tokens, "ln_gain": ln_gain, "w_branch": w_branch, "w_outgate": w_outgate, "w_gates": w_gates, "forget_bias": forget_bias, "conv_weight": conv_weight, "conv_bias": conv_bias, "w_query": w_query, "w_key": w_key, "w_value": w_value, "skip_gain": skip_gain, "norm_gain": norm_gain, "w_down": w_down, "lengths": lengths, "request_prompt": request_prompt}


EPSILON = 1e-05
GATE_CAP = 15.0
ROW_DIMS = (((0,), (0,)), ((), ()))
FEATURE_DIMS = (((1,), (1,)), ((), ()))

def norm_rows(source, gain_row):
    widened = source.astype(jnp.float32)
    row_mean = lax.optimization_barrier(jnp.mean(widened, axis=1, keepdims=True))
    row_var = lax.optimization_barrier(jnp.mean(widened * widened, axis=1, keepdims=True)) - row_mean * row_mean
    return ((widened - row_mean) * lax.rsqrt(row_var + EPSILON) * gain_row).astype(jnp.bfloat16)

def segment_of(positions, lengths):
    bound_one = lengths[0]
    bound_two = lengths[0] + lengths[1]
    return (positions >= bound_one).astype(jnp.int32) + (positions >= bound_two).astype(jnp.int32)

def conv_rows(extended, ext_segment, segment, weight, bias_row):
    row_count = segment.shape[0]
    widened = extended.astype(jnp.float32)
    summed = jnp.zeros((row_count, widened.shape[1]), jnp.float32) + bias_row
    for back_step in range(weight.shape[0]):
        low_row = weight.shape[0] - 1 - back_step
        keep_row = (ext_segment[low_row:low_row + row_count] == segment).astype(jnp.float32)
        summed = summed + weight[back_step] * widened[low_row:low_row + row_count] * keep_row[:, None]
    return jax.nn.silu(summed).astype(jnp.bfloat16)

def block_mix(source, weight):
    row_count = source.shape[0]
    grouped = source.astype(jnp.float32).reshape(row_count, 4, -1)
    mixed = jnp.einsum('tig,ijg->tjg', grouped, weight.astype(jnp.float32), precision=lax.Precision.HIGHEST)
    return mixed.reshape(row_count, -1)

def block_terms(queries, key_rows, values, log_forget, in_gate, segment, prev_seg):
    row_count = queries.shape[0]
    cum_log = jnp.cumsum(log_forget)
    row_order = jnp.arange(row_count)
    allowed = (row_order[:, None] >= row_order[None, :]) & (segment[:, None] == segment[None, :])
    exponent = jnp.where(allowed, cum_log[:, None] - cum_log[None, :] + in_gate[None, :], -jnp.inf)
    scores = lax.dot_general(queries, key_rows, FEATURE_DIMS, preferred_element_type=jnp.float32) * jnp.exp(exponent)
    in_block = jnp.dot(scores.astype(jnp.bfloat16), values, preferred_element_type=jnp.float32)
    carried = jnp.where(segment == prev_seg, jnp.exp(cum_log), 0.0)
    last_seg = segment[row_count - 1]
    weights = jnp.where(segment == last_seg, jnp.exp(cum_log[row_count - 1] - cum_log + in_gate), 0.0)
    weighted = (key_rows.astype(jnp.float32) * weights[:, None]).astype(jnp.bfloat16)
    increment = lax.dot_general(weighted, values, ROW_DIMS, preferred_element_type=jnp.float32)
    block_decay = jnp.where(last_seg == prev_seg, jnp.exp(cum_log[row_count - 1]), 0.0)
    return (in_block, carried, increment, block_decay)

def end_state(state_in, key_rows, values, cum_log, in_gate, segment, seg_before, local_end, prompt, holder):
    end_cum = cum_log[local_end]
    entering = jnp.where(holder & (seg_before == prompt), jnp.exp(end_cum), 0.0)
    row_order = jnp.arange(segment.shape[0])
    chosen = holder & (segment == prompt) & (row_order <= local_end)
    weights = jnp.where(chosen, jnp.exp(end_cum - cum_log + in_gate), 0.0)
    weighted = (key_rows.astype(jnp.float32) * weights[:, None]).astype(jnp.bfloat16)
    return entering * state_in + lax.dot_general(weighted, values, ROW_DIMS, preferred_element_type=jnp.float32)

def mlstm_head(queries, key_rows, values, log_forget, in_gate, segment):
    block_count = queries.shape[0] // BLK
    seg_blocks = segment.reshape(block_count, BLK)
    prev_segs = jnp.concatenate([jnp.full((1,), -1, jnp.int32), seg_blocks[:-1, BLK - 1]])

    def advance(state_now, inputs):
        block_queries, block_keys, block_values, block_log, block_gate, block_seg, prev_seg = inputs
        in_block, carried, increment, block_decay = block_terms(block_queries, block_keys, block_values, block_log, block_gate, block_seg, prev_seg)
        hidden = in_block + carried[:, None] * jnp.dot(block_queries, state_now.astype(jnp.bfloat16), preferred_element_type=jnp.float32)
        return (block_decay * state_now + increment, (hidden, state_now))
    initial = jnp.zeros((key_rows.shape[1], values.shape[1]), jnp.float32)
    final_carry, (hidden, block_states) = lax.scan(advance, initial, (queries.reshape(block_count, BLK, -1), key_rows.reshape(block_count, BLK, -1), values.reshape(block_count, BLK, -1), log_forget.reshape(block_count, BLK), in_gate.reshape(block_count, BLK), seg_blocks, prev_segs))
    return (hidden.reshape(queries.shape[0], values.shape[1]), block_states)

def reference(tokens, ln_gain, w_branch, w_outgate, w_gates, forget_bias, conv_weight, conv_bias, w_query, w_key, w_value, skip_gain, norm_gain, w_down, lengths, request_prompt):
    total_rows = tokens.shape[0]
    positions = jnp.arange(total_rows, dtype=jnp.int32)
    segment = segment_of(positions, lengths)
    ext_segment = jnp.concatenate([jnp.full((CONV - 1,), -1, jnp.int32), segment])
    prompt_starts = [jnp.zeros((), jnp.int32), lengths[0], lengths[0] + lengths[1]]
    prompt_ends = [lengths[0] - 1, lengths[0] + lengths[1] - 1, jnp.zeros((), jnp.int32) + (total_rows - 1)]
    head_width = INNER // HEADS
    slab_width = INNER // (N_WR * N_WC)
    dev_blocks = TOK_DEV // BLK
    current = tokens
    state_layers = []
    edge_layers = []
    for layer_idx in range(LAYERS):
        normed = norm_rows(current, ln_gain[layer_idx])
        branch = jnp.dot(normed, w_branch[layer_idx], preferred_element_type=jnp.float32).astype(jnp.bfloat16)
        outgate = jnp.dot(normed, w_outgate[layer_idx], preferred_element_type=jnp.float32)
        gate_pre = jnp.dot(normed, w_gates[layer_idx], preferred_element_type=jnp.float32)
        padded_branch = jnp.concatenate([jnp.zeros((CONV - 1, INNER), jnp.bfloat16), branch], axis=0)
        conv_act = conv_rows(padded_branch, ext_segment, segment, conv_weight[layer_idx], conv_bias[layer_idx])
        normal_heads = []
        prompt_states = [[] for prompt in range(PROMPTS)]
        for head_idx in range(HEADS):
            lo_col = head_idx * head_width
            hi_col = lo_col + head_width
            queries = block_mix(conv_act[:, lo_col:hi_col], w_query[layer_idx, head_idx]).astype(jnp.bfloat16)
            key_rows = (block_mix(conv_act[:, lo_col:hi_col], w_key[layer_idx, head_idx]) * head_width ** (-0.5)).astype(jnp.bfloat16)
            values = block_mix(branch[:, lo_col:hi_col], w_value[layer_idx, head_idx]).astype(jnp.bfloat16)
            in_gate = GATE_CAP * jnp.tanh(gate_pre[:, head_idx] / GATE_CAP)
            log_forget = jax.nn.log_sigmoid(gate_pre[:, HEADS + head_idx] + forget_bias[layer_idx, head_idx])
            hidden, block_states = mlstm_head(queries, key_rows, values, log_forget, in_gate, segment)
            sums_one = lax.optimization_barrier(jnp.sum(hidden, axis=1))
            sums_two = lax.optimization_barrier(jnp.sum(hidden * hidden, axis=1))
            row_mean = sums_one / head_width
            row_var = sums_two / head_width - row_mean * row_mean
            normal_heads.append((hidden - row_mean[:, None]) * lax.rsqrt(row_var + EPSILON)[:, None])
            for prompt in range(PROMPTS):
                end_pos = prompt_ends[prompt]
                device = end_pos // TOK_DEV
                dev_start = (device * TOK_DEV).astype(jnp.int32)
                state_in = block_states[device * dev_blocks]
                seg_before = jnp.where(dev_start > 0, segment[jnp.maximum(dev_start - 1, 0)], -1)
                part_log = lax.dynamic_slice_in_dim(log_forget, dev_start, TOK_DEV, 0)
                part_gate = lax.dynamic_slice_in_dim(in_gate, dev_start, TOK_DEV, 0)
                part_seg = lax.dynamic_slice_in_dim(segment, dev_start, TOK_DEV, 0)
                part_keys = lax.dynamic_slice_in_dim(key_rows, dev_start, TOK_DEV, 0)
                part_values = lax.dynamic_slice_in_dim(values, dev_start, TOK_DEV, 0)
                cum_log = jnp.cumsum(part_log)
                holder = end_pos >= dev_start
                prompt_states[prompt].append(end_state(state_in, part_keys, part_values, cum_log, part_gate, part_seg, seg_before, (end_pos - dev_start).astype(jnp.int32), prompt, holder))
        normal_all = jnp.concatenate(normal_heads, axis=1)
        gated = ((normal_all * norm_gain[layer_idx] + skip_gain[layer_idx] * conv_act.astype(jnp.float32)) * jax.nn.silu(outgate)).astype(jnp.bfloat16)
        accum = jnp.zeros((total_rows, D), jnp.float32)
        for block_idx in range(N_WR * N_WC):
            lo_row = block_idx * slab_width
            product = jnp.dot(gated[:, lo_row:lo_row + slab_width], w_down[layer_idx, lo_row:lo_row + slab_width], preferred_element_type=jnp.float32)
            rounded = lax.optimization_barrier(product.astype(jnp.bfloat16))
            accum = accum + rounded.astype(jnp.float32)
        current = (current.astype(jnp.float32) + accum).astype(jnp.bfloat16)
        finals = jnp.stack([jnp.stack(prompt_states[prompt]) for prompt in range(PROMPTS)]).astype(jnp.bfloat16)
        edges = []
        for prompt in range(PROMPTS):
            end_pos = prompt_ends[prompt]
            window = lax.dynamic_slice_in_dim(padded_branch, (end_pos + 1).astype(jnp.int32), CONV - 1, 0)
            edge_pos = end_pos - (CONV - 2) + jnp.arange(CONV - 1, dtype=jnp.int32)
            edges.append(jnp.where((edge_pos >= prompt_starts[prompt])[:, None], window, jnp.zeros_like(window)))
        edge_stack = jnp.stack(edges)
        state_layers.append(jnp.take(finals, request_prompt, axis=0))
        edge_layers.append(jnp.take(edge_stack, request_prompt, axis=0))
    return (current, jnp.stack(state_layers), jnp.stack(edge_layers))
```

```python
import jax
import jax.numpy as jnp
from jax import lax
from jax.sharding import PartitionSpec as P

HEADS = 4
CONV = 4
LAYERS = 2
PROMPTS = 3


EPSILON = 1e-05
GATE_CAP = 15.0
ROW_DIMS = (((0,), (0,)), ((), ()))
FEATURE_DIMS = (((1,), (1,)), ((), ()))


def shifted(value, axis, steps):
    count = lax.axis_size(axis)
    first, last = (max(0, -steps), min(count, count - steps))
    return lax.ppermute(value, axis, [(source, source + steps) for source in range(first, last)])


def span_weights(gathered, lengths, rows, count):
    spans = jnp.arange(count, dtype=jnp.int32)
    seg_end = segment_of(spans * rows + (rows - 1), lengths)
    totals = gathered[:, 0]
    later = jnp.arange(count + 1, dtype=jnp.int32)
    between = (spans[None, None, :] > spans[None, :, None]) & (
        spans[None, None, :] < later[:, None, None]
    )
    logs = jnp.sum(jnp.where(between, totals[None, None, :], 0.0), axis=2)
    seg_in = segment_of(later * rows - 1, lengths)
    keep = (spans[None, :] < later[:, None]) & (seg_end[None, :] == seg_in[:, None])
    state_rows = jnp.where(keep, jnp.exp(logs), 0.0)
    end_rows = []
    for prompt, end_pos in enumerate((lengths[0] - 1, lengths[0] + lengths[1] - 1)):
        holder = end_pos // rows
        pick = (spans == holder).astype(jnp.float32)
        end_cum = jnp.sum(pick * gathered[:, 1 + prompt])
        row = jnp.sum(pick[:, None] * logs[:count], axis=0) + end_cum
        kept = (spans < holder) & (seg_end == prompt)
        kept = kept & (segment_of(holder * rows - 1, lengths) == prompt)
        end_rows.append(jnp.where(kept, jnp.exp(row), 0.0))
    return state_rows[:count], jnp.stack(end_rows + [state_rows[count]])


def mix_spans(weights, spans):
    return jnp.sum(weights[:, :, None, None] * spans[None], axis=1)


def norm_rows(source, gain_row):
    widened = source.astype(jnp.float32)
    row_mean = jnp.mean(widened, axis=1, keepdims=True)
    row_var = jnp.mean(widened * widened, axis=1, keepdims=True) - row_mean * row_mean
    return ((widened - row_mean) * lax.rsqrt(row_var + EPSILON) * gain_row).astype(jnp.bfloat16)


def segment_of(positions, lengths):
    bound_one = lengths[0]
    bound_two = lengths[0] + lengths[1]
    return (positions >= bound_one).astype(jnp.int32) + (positions >= bound_two).astype(jnp.int32)


def conv_rows(extended, ext_segment, segment, weight, bias_row):
    row_count = segment.shape[0]
    widened = extended.astype(jnp.float32)
    summed = jnp.zeros((row_count, widened.shape[1]), jnp.float32) + bias_row
    for back_step in range(weight.shape[0]):
        low_row = weight.shape[0] - 1 - back_step
        keep_row = (ext_segment[low_row : low_row + row_count] == segment).astype(jnp.float32)
        summed = (
            summed + weight[back_step] * widened[low_row : low_row + row_count] * keep_row[:, None]
        )
    return jax.nn.silu(summed).astype(jnp.bfloat16)


def block_mix(source, weight):
    row_count = source.shape[0]
    grouped = source.astype(jnp.float32).reshape(row_count, 4, -1)
    mixed = jnp.einsum("tig,ijg->tjg", grouped, weight, precision=lax.Precision.HIGHEST)
    return mixed.reshape(row_count, -1)


def block_terms(queries, key_rows, values, log_forget, in_gate, segment, prev_seg):
    row_count = queries.shape[0]
    cum_log = jnp.cumsum(log_forget)
    row_order = jnp.arange(row_count)
    allowed = (row_order[:, None] >= row_order[None, :]) & (segment[:, None] == segment[None, :])
    exponent = jnp.where(allowed, cum_log[:, None] - cum_log[None, :] + in_gate[None, :], -jnp.inf)
    scores = lax.dot_general(
        queries, key_rows, FEATURE_DIMS, preferred_element_type=jnp.float32
    ) * jnp.exp(exponent)
    in_block = jnp.dot(scores.astype(jnp.bfloat16), values, preferred_element_type=jnp.float32)
    carried = jnp.where(segment == prev_seg, jnp.exp(cum_log), 0.0)
    last_seg = segment[row_count - 1]
    weights = jnp.where(
        segment == last_seg, jnp.exp(cum_log[row_count - 1] - cum_log + in_gate), 0.0
    )
    weighted = (key_rows.astype(jnp.float32) * weights[:, None]).astype(jnp.bfloat16)
    increment = lax.dot_general(weighted, values, ROW_DIMS, preferred_element_type=jnp.float32)
    return (in_block, carried, increment)


def end_part(key_rows, values, cum_log, in_gate, segment, local_end, prompt, holder):
    row_order = jnp.arange(segment.shape[0])
    chosen = holder & (segment == prompt) & (row_order <= local_end)
    weights = jnp.where(chosen, jnp.exp(cum_log[local_end] - cum_log + in_gate), 0.0)
    weighted = (key_rows.astype(jnp.float32) * weights[:, None]).astype(jnp.bfloat16)
    return lax.dot_general(weighted, values, ROW_DIMS, preferred_element_type=jnp.float32)


def body(
    tokens,
    ln_gain,
    w_branch,
    w_outgate,
    w_gates,
    forget_bias,
    conv_weight,
    conv_bias,
    w_query,
    w_key,
    w_value,
    skip_gain,
    norm_gain,
    w_down,
    lengths,
    request_prompt,
):
    tok_rows = tokens.shape[0]
    seq_count = lax.axis_size("seq")
    seq_index = lax.axis_index("seq")
    head_idx = lax.axis_index("wr")
    row_offset = seq_index * tok_rows
    total_rows = tok_rows * seq_count
    row_ids = jnp.arange(tok_rows, dtype=jnp.int32)
    positions = row_offset + row_ids
    segment = segment_of(positions, lengths)
    seg_before = jnp.where(row_offset > 0, segment_of(row_offset - 1, lengths), -1)
    rim_positions = row_offset - (CONV - 1) + jnp.arange(CONV - 1, dtype=jnp.int32)
    rim_segment = jnp.where(rim_positions >= 0, segment_of(rim_positions, lengths), -1)
    ext_segment = jnp.concatenate([rim_segment, segment])
    prompt_starts = [jnp.zeros((), jnp.int32), lengths[0], lengths[0] + lengths[1]]
    prompt_ends = [
        lengths[0] - 1,
        lengths[0] + lengths[1] - 1,
        jnp.zeros((), jnp.int32) + (total_rows - 1),
    ]
    head_mask = (jnp.arange(HEADS, dtype=jnp.int32) == head_idx).astype(jnp.float32)
    current = tokens
    sent_states = []
    sent_edges = []
    for layer_idx in range(LAYERS):
        gathered = lax.all_gather(current, ("wr", "wc"), axis=1, tiled=True)
        normed = norm_rows(gathered, ln_gain[layer_idx])
        branch = jnp.dot(normed, w_branch[layer_idx], preferred_element_type=jnp.float32).astype(
            jnp.bfloat16
        )
        outgate = jnp.dot(normed, w_outgate[layer_idx], preferred_element_type=jnp.float32)
        gate_pre = jnp.dot(normed, w_gates[layer_idx], preferred_element_type=jnp.float32)
        input_pre = jnp.sum(gate_pre[:, :HEADS] * head_mask, axis=1)
        forget_pre = jnp.sum((gate_pre[:, HEADS:] + forget_bias[layer_idx]) * head_mask, axis=1)
        in_gate = GATE_CAP * jnp.tanh(input_pre / GATE_CAP)
        log_forget = jax.nn.log_sigmoid(forget_pre)
        edge_in = shifted(branch[tok_rows - (CONV - 1) :], "seq", 1)
        extended = jnp.concatenate([edge_in, branch], axis=0)
        conv_act = conv_rows(
            extended, ext_segment, segment, conv_weight[layer_idx], conv_bias[layer_idx]
        )
        head_branch, head_act = (
            lax.all_gather(branch, "wc", axis=1, tiled=True),
            lax.all_gather(conv_act, "wc", axis=1, tiled=True),
        )
        head_width = head_act.shape[1]
        queries = block_mix(head_act, w_query[layer_idx, 0]).astype(jnp.bfloat16)
        key_rows = (block_mix(head_act, w_key[layer_idx, 0]) * head_width ** (-0.5)).astype(
            jnp.bfloat16
        )
        values = block_mix(head_branch, w_value[layer_idx, 0]).astype(jnp.bfloat16)
        cum_log = jnp.cumsum(log_forget)
        holders = [
            (end_pos >= row_offset) & (end_pos < row_offset + tok_rows) for end_pos in prompt_ends
        ]
        local_ends = [jnp.clip(end_pos - row_offset, 0, tok_rows - 1) for end_pos in prompt_ends]
        span_logs = lax.all_gather(
            jnp.stack([cum_log[tok_rows - 1], cum_log[local_ends[0]], cum_log[local_ends[1]]]),
            "seq",
        )
        state_rows, end_rows = span_weights(span_logs, lengths, tok_rows, seq_count)
        in_block, carried, increment = block_terms(
            queries, key_rows, values, log_forget, in_gate, segment, seg_before
        )
        parts = [increment] + [
            end_part(
                key_rows,
                values,
                cum_log,
                in_gate,
                segment,
                local_ends[prompt],
                prompt,
                holders[prompt],
            )
            for prompt in range(PROMPTS - 1)
        ]
        slab = head_width // seq_count
        sent = jnp.stack(
            [part.astype(jnp.bfloat16).reshape(seq_count, slab, -1) for part in parts], axis=1
        )
        got = lax.all_to_all(sent, "seq", 0, 0, tiled=True).astype(jnp.float32)
        spans = got[:, 0]
        states = mix_spans(state_rows, spans).astype(jnp.bfloat16)
        state_here = lax.all_to_all(states, "seq", 0, 0, tiled=True).reshape(head_width, -1)
        own_ends = jnp.sum(got[:, 1:], axis=0)
        ends = mix_spans(end_rows, spans) + jnp.concatenate(
            [own_ends, jnp.zeros_like(own_ends[:1])], axis=0
        )
        sent_states.append(
            lax.all_gather(ends.astype(jnp.bfloat16), "seq", axis=1, tiled=True)
        )
        hidden_parts = in_block + carried[:, None] * jnp.dot(
            queries, state_here, preferred_element_type=jnp.float32
        )
        sums_one, sums_two = lax.psum(
            (jnp.sum(hidden_parts, axis=1), jnp.sum(hidden_parts * hidden_parts, axis=1)), "wc"
        )
        row_mean = sums_one / head_width
        row_var = sums_two / head_width - row_mean * row_mean
        normal_rows = (hidden_parts - row_mean[:, None]) * lax.rsqrt(row_var + EPSILON)[:, None]
        gated = (
            (
                normal_rows * norm_gain[layer_idx]
                + skip_gain[layer_idx] * conv_act.astype(jnp.float32)
            )
            * jax.nn.silu(outgate)
        ).astype(jnp.bfloat16)
        term_rows = jnp.dot(gated, w_down[layer_idx], preferred_element_type=jnp.float32)
        terms = lax.all_to_all(
            term_rows.astype(jnp.bfloat16), ("wr", "wc"), 1, 0, tiled=True
        ).reshape(-1, tok_rows, current.shape[1])
        summed = jnp.sum(terms.astype(jnp.float32), axis=0)
        current = (current.astype(jnp.float32) + summed).astype(jnp.bfloat16)
        for prompt in range(PROMPTS):
            window = lax.dynamic_slice_in_dim(extended, local_ends[prompt] + 1, CONV - 1, 0)
            edge_pos = (
                prompt_ends[prompt] - (CONV - 2) + jnp.arange(CONV - 1, dtype=jnp.int32)
            )
            sent_edges.append(
                jnp.where(
                    ((edge_pos >= prompt_starts[prompt]) & holders[prompt])[:, None],
                    window,
                    jnp.zeros_like(window),
                )
            )
    state_stack = jnp.stack(sent_states)
    edge_stack = lax.psum(jnp.stack(sent_edges), "seq")
    edge_stack = edge_stack.reshape(LAYERS, PROMPTS, edge_stack.shape[1], edge_stack.shape[2])
    chooser = (request_prompt[:, None] == jnp.arange(PROMPTS, dtype=jnp.int32)[None, :]).astype(
        jnp.bfloat16
    )
    request_state = jnp.einsum(
        "rp,lphd->lrhd", chooser, state_stack, preferred_element_type=jnp.float32
    ).astype(jnp.bfloat16)[:, :, None]
    request_conv = jnp.einsum(
        "rp,lpkc->lrkc", chooser, edge_stack, preferred_element_type=jnp.float32
    ).astype(jnp.bfloat16)
    return (current, request_state, request_conv)


def solution(mesh):
    return jax.shard_map(
        body,
        mesh=mesh,
        in_specs=(
            P("seq", ("wr", "wc")),
            P(),
            P(None, None, ("wr", "wc")),
            P(None, None, ("wr", "wc")),
            P(),
            P(),
            P(None, None, ("wr", "wc")),
            P(None, ("wr", "wc")),
            P(None, "wr", None, None, None),
            P(None, "wr", None, None, None),
            P(None, "wr", None, "wc", None),
            P(None, ("wr", "wc")),
            P(None, ("wr", "wc")),
            P(None, ("wr", "wc"), None),
            P(),
            P("seq"),
        ),
        out_specs=(
            P("seq", ("wr", "wc")),
            P(None, "seq", "wr", None, "wc"),
            P(None, "seq", None, ("wr", "wc")),
        ),
        check_vma=False,
    )
```
